512 devices in a mesh: segment: 64 (over z, y_hi, core), tensor: 8 (over y_lo, x).
Axes of the slice: x: 4, y: 4 (y_hi: 2, y_lo: 2; y = y_hi * 2 + y_lo), z: 16, core: 2. Of those that a mesh axis runs over, the one named last changes fastest.
Arguments:
- queries: bfloat16 [64, 256, 8192], P('segment', None, 'tensor'), may hold values from -36 to 36
- prompt_keys: bfloat16 [64, 4096, 1024], P('segment', None, 'tensor'), may hold values from -6.75 to 6.75
- prompt_values: bfloat16 [64, 4096, 1024], P('segment', None, 'tensor'), may hold values from -24 to 24
- tree_keys: bfloat16 [64, 256, 1024], P('segment', None, 'tensor'), may hold values from -18 to 18
- tree_values: bfloat16 [64, 256, 1024], P('segment', None, 'tensor'), may hold values from -24 to 24
- tree_mask: int32 [64, 4, 64, 64], P('segment'), may hold values 0 or 1
Outputs:
- handed_on: bfloat16 [64, 256, 8192], P('segment')
The draws below stay inside these ranges and needn't reach their ends.
All inputs are finite; a program needn't handle non-finite values. No bound on the sum of `tree_mask` on one device may be relied on, other than what follows from the above.
Results may differ from the reference program's by a relative error of at most 0.006.
Values may be sent and summed in bfloat16 or wider, within the bound.
No kernel may reach another device: no remote copies, remote signals or barrier semaphores. Data moves between devices by JAX's collectives and lax.ppermute only.
A program may use at most 64 MiB of HBM per device.

```python
import jax
import jax.numpy as jnp
from jax import lax

HEADS = 64
KV_HEADS = 8
HEAD_DIM = 128
TREE = 64
MB_DEV = 4
PROMPT = 4096
GROUP = 8
ROWS = 256
SEGMENTS = 64


def prompt_key_field(key):
    key_base = jax.random.normal(jax.random.fold_in(key, 11), (SEGMENTS, PROMPT, KV_HEADS * HEAD_DIM), jnp.float32)
    key_base = jnp.clip(key_base, -3.0, 3.0) * 2.0
    return key_base


def draw_prompt_keys(key, part):
    return prompt_key_field(key).astype(jnp.bfloat16)


def draw_queries(key, part):
    query_noise = jax.random.normal(jax.random.fold_in(key, 23), (SEGMENTS, ROWS, HEADS * HEAD_DIM), jnp.float32)
    query_noise = jnp.clip(query_noise, -4.0, 4.0)
    return query_noise.astype(jnp.bfloat16)


def plant(result, own_key, low, high):
    index_at = [jax.random.randint(jax.random.fold_in(own_key, axis), (), 0, length) for axis, length in enumerate(result.shape)]
    widest = result.shape.index(max(result.shape))
    beside = index_at[:widest] + [(index_at[widest] + 1) % result.shape[widest]] + index_at[widest + 1:]
    return result.at[tuple(index_at)].set(low).at[tuple(beside)].set(high)


def steps_of(key, extent, cuts, smallest, largest):
    gain = 1.0
    for position, blocks in cuts:
        steps = jax.random.uniform(jax.random.fold_in(jax.random.fold_in(key, 6), position), (blocks,), jnp.float32, smallest / len(cuts), largest / len(cuts))
        gain = gain * jnp.repeat(jnp.exp(steps), extent[position] // blocks).reshape((-1,) + (1,) * (len(extent) - 1 - position))
    return gain


def noise(key, shape, scale, reach, cuts=(), held_as=jnp.bfloat16):
    drawn = jax.random.normal(key, shape, jnp.float32) * scale
    if len(cuts) > 0:
        drawn = steps_of(key, shape, cuts, -0.22, 0.18) * drawn
    return jnp.clip(drawn, min=-reach, max=reach).astype(held_as)


def setup_inputs(seed: int = 0) -> dict:
    keys = jax.random.split(jax.random.key(seed), 7)
    return {
        "queries": draw_queries(jax.random.fold_in(keys[6], 71), 0),
        "prompt_keys": draw_prompt_keys(jax.random.fold_in(keys[6], 71), 0),
        "prompt_values": noise(keys[2], (SEGMENTS, PROMPT, KV_HEADS * HEAD_DIM), 4.0, 24.0, ((0, 64), (2, 8))),
        "tree_keys": noise(keys[3], (SEGMENTS, ROWS, KV_HEADS * HEAD_DIM), 3.0, 18.0, ((0, 64), (2, 8))),
        "tree_values": noise(keys[4], (SEGMENTS, ROWS, KV_HEADS * HEAD_DIM), 4.0, 24.0, ((0, 64), (2, 8))),
        "tree_mask": plant((jax.random.randint(keys[5], (SEGMENTS, MB_DEV, TREE, TREE), 0, 2) < 1).astype(jnp.int32), jax.random.fold_in(keys[5], 1), 0, 1),
    }


def rounded(values):
    return lax.optimization_barrier(values.astype(jnp.bfloat16)).astype(jnp.float32)


def attend_segment(pieces):
    query_part, key_part, value_part, tree_key_part, tree_value_part, visible_mask = pieces
    score_scale = HEAD_DIM ** -0.5
    query_float = query_part.astype(jnp.float32).reshape(MB_DEV, TREE, KV_HEADS, GROUP, HEAD_DIM)
    key_float = key_part.astype(jnp.float32).reshape(PROMPT, KV_HEADS, HEAD_DIM)
    value_float = value_part.astype(jnp.float32).reshape(PROMPT, KV_HEADS, HEAD_DIM)
    tree_key_float = tree_key_part.astype(jnp.float32).reshape(MB_DEV, TREE, KV_HEADS, HEAD_DIM)
    tree_value_float = tree_value_part.astype(jnp.float32).reshape(MB_DEV, TREE, KV_HEADS, HEAD_DIM)
    prompt_scores = jnp.einsum("mtkgd,pkd->mtkgp", query_float, key_float) * score_scale
    tree_scores = jnp.einsum("mtkgd,mjkd->mtkgj", query_float, tree_key_float) * score_scale
    seen = (visible_mask == 1)[:, :, None, None, :]
    tree_scores = jnp.where(seen, tree_scores, -jnp.inf)
    highest = jnp.maximum(jnp.max(prompt_scores, axis=-1), jnp.max(tree_scores, axis=-1))[..., None]
    prompt_exp = jnp.exp(prompt_scores - highest)
    tree_exp = jnp.exp(tree_scores - highest)
    totals = jnp.sum(prompt_exp, axis=-1) + jnp.sum(tree_exp, axis=-1)
    summed = jnp.einsum("mtkgp,pkd->mtkgd", rounded(prompt_exp), value_float)
    summed = summed + jnp.einsum("mtkgj,mjkd->mtkgd", rounded(tree_exp), tree_value_float)
    attended = (summed / totals[..., None]).astype(jnp.bfloat16)
    return attended.reshape(ROWS, HEADS * HEAD_DIM)


def reference(queries, prompt_keys, prompt_values, tree_keys, tree_values, tree_mask):
    attended = lax.map(attend_segment, (queries, prompt_keys, prompt_values, tree_keys, tree_values, tree_mask))
    return jnp.roll(attended, 1, axis=0)
```

```python
import functools

import jax
import jax.numpy as jnp
from jax import lax
from jax.experimental import pallas as pl
from jax.experimental.pallas import tpu as pltpu
from jax.sharding import PartitionSpec as P

HEAD_DIM = 128
TREE = 64
PROMPT = 4096
GROUP = 8
WIDTH = GROUP * HEAD_DIM
EXP2_SCALE = 1.4426950408889634 * HEAD_DIM ** (-0.5)
TILE = 256
KEY_BLOCK = 512
CHUNKS = ((0, 64), (64, 64), (128, 64), (192, 64))


def matmul_nt(a, b):
    return lax.dot_general(a, b, (((1,), (1,)), ((), ())), preferred_element_type=jnp.float32)


def attend_kernel(first, rows, q_ref, k_ref, v_ref, tk_ref, tv_ref, mask_ref, o_ref, stacked, score, wide):
    total_rows = GROUP * rows
    tiles = total_rows // TILE
    blocks = PROMPT // KEY_BLOCK
    heads = TILE // rows
    batch = first // TREE
    inside = first - batch * TREE
    for g in range(GROUP):
        stacked[g * rows : (g + 1) * rows, :] = q_ref[0, first : first + rows, g * HEAD_DIM : (g + 1) * HEAD_DIM]
    wide[:, :HEAD_DIM] = v_ref[0]
    wide[:, HEAD_DIM:] = jnp.ones((PROMPT, HEAD_DIM), jnp.bfloat16)
    seen = mask_ref[0, batch, inside : inside + rows, :]
    seen = jnp.concatenate([seen] * heads, axis=0) == 1
    tree_keys = tk_ref[0, batch * TREE : (batch + 1) * TREE, :]
    tree_values = tv_ref[0, batch * TREE : (batch + 1) * TREE, :]

    ready = None
    for t in range(tiles + 1):
        peak = None
        summed = None
        for b in range(blocks):
            keys = slice(b * KEY_BLOCK, (b + 1) * KEY_BLOCK)
            if t < tiles:
                s = matmul_nt(stacked[t * TILE : (t + 1) * TILE, :], k_ref[0, keys, :])
                score[t % 2, :, keys] = s
                for i in range(KEY_BLOCK // 128):
                    part = s[:, i * 128 : (i + 1) * 128]
                    peak = part if peak is None else jnp.maximum(peak, part)
            if t > 0:
                weights = jnp.exp2(score[(t - 1) % 2, :, keys] * EXP2_SCALE - ready[1]).astype(jnp.bfloat16)
                part = jnp.dot(weights, wide[keys, :], preferred_element_type=jnp.float32)
                summed = part if summed is None else summed + part
        if t > 0:
            tree_scores, highest = ready
            tree_exp = jnp.exp2(tree_scores * EXP2_SCALE - highest)
            totals = summed[:, HEAD_DIM:] + jnp.sum(tree_exp, axis=-1, keepdims=True)
            attended = summed[:, :HEAD_DIM] + jnp.dot(
                tree_exp.astype(jnp.bfloat16), tree_values, preferred_element_type=jnp.float32
            )
            attended = (attended / totals).astype(jnp.bfloat16)
            for i in range(heads):
                g = (t - 1) * heads + i
                o_ref[0, :, g * HEAD_DIM : (g + 1) * HEAD_DIM] = attended[i * rows : (i + 1) * rows]
        if t < tiles:
            tree_scores = matmul_nt(stacked[t * TILE : (t + 1) * TILE, :], tree_keys)
            tree_scores = jnp.where(seen, tree_scores, -jnp.inf)
            highest = jnp.maximum(
                jnp.max(peak, axis=-1, keepdims=True), jnp.max(tree_scores, axis=-1, keepdims=True)
            )
            ready = (tree_scores, highest * EXP2_SCALE)


def attend(arrays, first, rows):
    whole = pl.BlockSpec(memory_space=pltpu.VMEM)
    total_rows = GROUP * rows
    return pl.pallas_call(
        functools.partial(attend_kernel, first, rows),
        out_shape=jax.ShapeDtypeStruct((1, rows, WIDTH), jnp.bfloat16),
        in_specs=[whole] * 6,
        out_specs=whole,
        scratch_shapes=[
            pltpu.VMEM((total_rows, HEAD_DIM), jnp.bfloat16),
            pltpu.VMEM((2, TILE, PROMPT), jnp.float32),
            pltpu.VMEM((PROMPT, 2 * HEAD_DIM), jnp.bfloat16),
        ],
        compiler_params=pltpu.CompilerParams(vmem_limit_bytes=24 * 2**20),
        cost_estimate=pl.CostEstimate(
            flops=4 * total_rows * PROMPT * HEAD_DIM,
            bytes_accessed=3 * 2**20,
            transcendentals=total_rows * PROMPT,
        ),
        name=f"attend_{first}_{rows}",
    )(*arrays)


def place_kernel(first, rows, pieces_ref, *refs):
    out_ref, sem = refs[-2:]
    flip = 4 * (1 - lax.rem(lax.axis_index("segment"), 2))
    copies = []
    for j in range(8):
        column = lax.rem(j + flip, 8) * WIDTH
        copies.append(
            pltpu.make_async_copy(
                pieces_ref.at[j, 0],
                out_ref.at[0, pl.ds(first, rows), pl.ds(pl.multiple_of(column, WIDTH), WIDTH)],
                sem.at[j],
            )
        )
    for copy in copies:
        copy.start()
    for copy in copies:
        copy.wait()


def place(pieces, out, first, rows):
    anywhere = pl.BlockSpec(memory_space=pl.ANY)
    operands = (pieces,) if out is None else (pieces, out)
    return pl.pallas_call(
        functools.partial(place_kernel, first, rows),
        out_shape=jax.ShapeDtypeStruct((1, 256, 8 * WIDTH), jnp.bfloat16),
        in_specs=[anywhere] * len(operands),
        out_specs=anywhere,
        scratch_shapes=[pltpu.SemaphoreType.DMA((8,))],
        input_output_aliases={} if out is None else {1: 0},
        cost_estimate=pl.CostEstimate(flops=0, bytes_accessed=2 * rows * 8 * WIDTH * 2, transcendentals=0),
        name=f"place_{first}_{rows}",
    )(*operands)


def relay(block):
    route = []
    for s in range(64):
        for t in range(8):
            target = t if s % 2 == 0 else t ^ 4
            route.append((s * 8 + t, ((s + 1) % 64) * 8 + target))
    return lax.ppermute(block, ("segment", "tensor"), route)


def body(*arrays):
    moved = []
    for first, rows in CHUNKS:
        attended = attend(arrays, first, rows)
        moved.append(relay(attended))
    out = None
    for (first, rows), block in zip(CHUNKS, moved):
        pieces = lax.all_to_all(jnp.broadcast_to(block[None], (8,) + block.shape), "tensor", 0, 0)
        out = place(pieces, out, first, rows)
    return out


def solution(mesh):
    placed = (
        P("segment", None, "tensor"),
        P("segment", None, "tensor"),
        P("segment", None, "tensor"),
        P("segment", None, "tensor"),
        P("segment", None, "tensor"),
        P("segment", None, None, None),
    )
    return jax.shard_map(
        body, mesh=mesh, in_specs=placed, out_specs=P("segment", None, None), check_vma=False
    )
```

```python
import functools

import jax
import jax.numpy as jnp
from jax import lax
from jax.experimental import pallas as pl
from jax.experimental.pallas import tpu as pltpu
from jax.sharding import PartitionSpec as P

HEAD_DIM = 128
TREE = 64
PROMPT = 4096
GROUP = 8
ROWS = 256
WIDTH = GROUP * HEAD_DIM
EXP2_SCALE = 1.4426950408889634 * HEAD_DIM ** (-0.5)
TILE = 256
KEY_BLOCK = 512
SHAPES = (
    (1, ROWS, WIDTH),
    (1, PROMPT, HEAD_DIM),
    (1, PROMPT, HEAD_DIM),
    (1, ROWS, HEAD_DIM),
    (1, ROWS, HEAD_DIM),
    (1, 4, TREE, TREE),
)
TYPES = (jnp.bfloat16,) * 5 + (jnp.int32,)


def matmul_nt(a, b):
    return lax.dot_general(a, b, (((1,), (1,)), ((), ())), preferred_element_type=jnp.float32)


def attend_rows(first, rows, held, o_ref, stacked, score, arrived):
    q_ref, k_ref, v_ref, tk_ref, tv_ref, mask_ref = held
    part_rows = TREE if rows % TREE == 0 else TREE // 2
    parts = rows // part_rows
    tiles = GROUP * rows // TILE
    per_part = tiles // parts
    blocks = PROMPT // KEY_BLOCK
    heads = TILE // part_rows
    copies = o_ref.shape[0]
    ones = jnp.ones((KEY_BLOCK, HEAD_DIM), jnp.bfloat16)
    arrived("queries")
    for p in range(parts):
        for g in range(GROUP):
            start = (p * GROUP + g) * part_rows
            row = first + p * part_rows
            stacked[start : start + part_rows, :] = q_ref[
                0, row : row + part_rows, g * HEAD_DIM : (g + 1) * HEAD_DIM
            ]

    ready = None
    for t in range(tiles + 1):
        peak = None
        summed = None
        for b in range(blocks):
            keys = slice(b * KEY_BLOCK, (b + 1) * KEY_BLOCK)
            if t < tiles:
                if t == 0:
                    arrived("keys", b)
                s = matmul_nt(stacked[t * TILE : (t + 1) * TILE, :], k_ref[0, keys, :])
                score[t % 2, :, keys] = s
                for i in range(KEY_BLOCK // 128):
                    piece = s[:, i * 128 : (i + 1) * 128]
                    peak = piece if peak is None else jnp.maximum(peak, piece)
            if t > 0:
                if t == 1 and b == 0:
                    arrived("values")
                weights = jnp.exp2(score[(t - 1) % 2, :, keys] * EXP2_SCALE - ready[1]).astype(jnp.bfloat16)
                wide = jnp.concatenate([v_ref[0, keys, :], ones], axis=1)
                piece = jnp.dot(weights, wide, preferred_element_type=jnp.float32)
                summed = piece if summed is None else summed + piece
        if t > 0:
            tree_scores, highest, batch = ready
            tree_exp = jnp.exp2(tree_scores * EXP2_SCALE - highest)
            totals = summed[:, HEAD_DIM:] + jnp.sum(tree_exp, axis=-1, keepdims=True)
            tree_values = tv_ref[0, batch * TREE : (batch + 1) * TREE, :]
            attended = summed[:, :HEAD_DIM] + jnp.dot(
                tree_exp.astype(jnp.bfloat16), tree_values, preferred_element_type=jnp.float32
            )
            attended = (attended / totals).astype(jnp.bfloat16)
            p, q = divmod(t - 1, per_part)
            for i in range(heads):
                g = q * heads + i
                for c in range(copies):
                    o_ref[c, p * part_rows : (p + 1) * part_rows, g * HEAD_DIM : (g + 1) * HEAD_DIM] = attended[
                        i * part_rows : (i + 1) * part_rows
                    ]
        if t < tiles:
            if t == 0:
                arrived("tree")
            row = first + (t // per_part) * part_rows
            batch = row // TREE
            inside = row - batch * TREE
            seen = mask_ref[0, batch, inside : inside + part_rows, :]
            seen = jnp.concatenate([seen] * heads, axis=0) == 1
            tree_keys = tk_ref[0, batch * TREE : (batch + 1) * TREE, :]
            tree_scores = matmul_nt(stacked[t * TILE : (t + 1) * TILE, :], tree_keys)
            tree_scores = jnp.where(seen, tree_scores, -jnp.inf)
            highest = jnp.maximum(
                jnp.max(peak, axis=-1, keepdims=True), jnp.max(tree_scores, axis=-1, keepdims=True)
            )
            ready = (tree_scores, highest * EXP2_SCALE, batch)


def attend_kernel(first, rows, loaded, *refs):
    o_ref, stacked, score = refs[6:9]
    held = list(refs[:6])
    copies = {}
    if loaded:
        sem = refs[-1]
        for i, buffer in zip(loaded, refs[9:]):
            held[i] = buffer
        count = 0
        for i in (0, 1, 3, 5, 2, 4):
            if i not in loaded:
                continue
            pieces = [(refs[i], held[i])]
            if i == 0:
                pieces = [(refs[0].at[:, pl.ds(first, rows)], held[0].at[:, pl.ds(first, rows)])]
            if i == 1:
                blocks = [pl.ds(b * KEY_BLOCK, KEY_BLOCK) for b in range(PROMPT // KEY_BLOCK)]
                pieces = [(refs[1].at[:, keys], held[1].at[:, keys]) for keys in blocks]
            for b, (source, target) in enumerate(pieces):
                copies[i, b] = pltpu.make_async_copy(source, target, sem.at[count])
                copies[i, b].start()
                count += 1

    def arrived(what, b=0):
        for i in {"queries": (0,), "keys": (1,), "tree": (3, 5), "values": (2, 4)}[what]:
            if (i, b) in copies:
                copies[i, b].wait()

    attend_rows(first, rows, held, o_ref, stacked, score, arrived)


def attend(arrays, first, rows, copies, loaded, limit):
    vmem = pl.BlockSpec(memory_space=pltpu.VMEM)
    total_rows = GROUP * rows
    scratch = [
        pltpu.VMEM((total_rows, HEAD_DIM), jnp.bfloat16),
        pltpu.VMEM((2, TILE, PROMPT), jnp.float32),
    ]
    scratch += [pltpu.VMEM(SHAPES[i], TYPES[i]) for i in loaded]
    if loaded:
        scratch.append(pltpu.SemaphoreType.DMA((5 + PROMPT // KEY_BLOCK,)))
    return pl.pallas_call(
        functools.partial(attend_kernel, first, rows, loaded),
        out_shape=jax.ShapeDtypeStruct((copies, rows, WIDTH), jnp.bfloat16),
        in_specs=[pl.BlockSpec(memory_space=pltpu.HBM) if i in loaded else vmem for i in range(6)],
        out_specs=vmem,
        scratch_shapes=scratch,
        compiler_params=pltpu.CompilerParams(vmem_limit_bytes=limit * 2**20),
        cost_estimate=pl.CostEstimate(
            flops=4 * total_rows * PROMPT * HEAD_DIM,
            bytes_accessed=3 * 2**20,
            transcendentals=total_rows * PROMPT,
        ),
        name=f"attend_{first}_{rows}",
    )(*arrays)


def place_kernel(first, rows, kinds, *refs):
    side_ref, pieces_ref, out_ref, sem = refs[0], refs[1], refs[-2], refs[-1]
    copies = []
    for k, kind in enumerate(kinds):
        for x in range(4):
            column = pl.multiple_of((lax.bitwise_xor(side_ref[0], kind) * 4 + x) * WIDTH, WIDTH)
            copies.append(
                pltpu.make_async_copy(
                    pieces_ref.at[x, k],
                    out_ref.at[0, pl.ds(first, rows), pl.ds(column, WIDTH)],
                    sem.at[len(copies)],
                )
            )
    for copy in copies:
        copy.start()
    for copy in copies:
        copy.wait()


def place(pieces, side, kinds, out, first, rows):
    operands = (side, pieces) if out is None else (side, pieces, out)
    return pl.pallas_call(
        functools.partial(place_kernel, first, rows, kinds),
        in_specs=[pl.BlockSpec(memory_space=pltpu.SMEM), pl.BlockSpec(memory_space=pltpu.VMEM)]
        + [pl.BlockSpec(memory_space=pl.ANY)] * (len(operands) - 2),
        out_specs=pl.BlockSpec(memory_space=pl.ANY),
        out_shape=jax.ShapeDtypeStruct((1, ROWS, 8 * WIDTH), jnp.bfloat16),
        scratch_shapes=[pltpu.SemaphoreType.DMA((4 * len(kinds),))],
        input_output_aliases={} if out is None else {2: 0},
        compiler_params=pltpu.CompilerParams(vmem_limit_bytes=4 * 2**20),
        cost_estimate=pl.CostEstimate(
            flops=0, bytes_accessed=16 * len(kinds) * rows * WIDTH, transcendentals=0
        ),
        name=f"place_{first}_{kinds[0]}",
    )(*operands)


def hand_on(block, kind):
    route = []
    for s in range(64):
        for t in range(8):
            route.append((s * 8 + t, ((s + 1) % 64) * 8 + (t if s % 2 == kind else t ^ 4)))
    return lax.ppermute(block, ("segment", "tensor"), route)


def near_side():
    y = lax.shift_right_logical(lax.axis_index("tensor"), 2)
    core = lax.bitwise_and(lax.axis_index("segment"), 1)
    return jnp.reshape(lax.bitwise_xor(lax.bitwise_xor(y, core), 1), (1,)).astype(jnp.int32)


X_GROUPS = ((0, 1, 2, 3), (4, 5, 6, 7))
CUT = 160


def spread_x(blocks):
    return lax.all_to_all(blocks, "tensor", 0, 0, axis_index_groups=X_GROUPS)


def both_sides(near, far):
    pair = jnp.concatenate([near, far], axis=0)
    return jnp.broadcast_to(pair[None], (4,) + pair.shape)


def body(*arrays):
    side = near_side()
    barrier = lax.optimization_barrier
    a1 = attend(arrays, 0, CUT, 4, (0, 1, 2, 3, 4, 5), 60)
    g1 = spread_x(a1)
    a2 = attend(arrays, CUT, ROWS - CUT, 1, (3, 4, 5), 24)
    n2, f2 = hand_on(a2, 0), hand_on(a2, 1)
    n1, f1 = hand_on(g1, 0), hand_on(g1, 1)
    g2 = spread_x(both_sides(n2, f2))
    out = place(n1[:, None], side, (0,), None, 0, CUT)
    out = place(f1[:, None], side, (1,), out, 0, CUT)
    out = place(g2, side, (0, 1), out, CUT, ROWS - CUT)
    return out


def solution(mesh):
    placed = (
        P("segment", None, "tensor"),
        P("segment", None, "tensor"),
        P("segment", None, "tensor"),
        P("segment", None, "tensor"),
        P("segment", None, "tensor"),
        P("segment", None, None, None),
    )
    return jax.shard_map(
        body, mesh=mesh, in_specs=placed, out_specs=P("segment", None, None), check_vma=False
    )
```

```python
import functools

import jax
import jax.numpy as jnp
from jax import lax
from jax.experimental import pallas as pl
from jax.experimental.pallas import tpu as pltpu
from jax.sharding import PartitionSpec as P

HEAD_DIM = 128
TREE = 64
PROMPT = 4096
GROUP = 8
ROWS = 256
WIDTH = GROUP * HEAD_DIM
EXP2_SCALE = 1.4426950408889634 * HEAD_DIM ** (-0.5)
TILE = 256
KEY_BLOCK = 512
SHAPES = (
    (1, ROWS, WIDTH),
    (1, PROMPT, HEAD_DIM),
    (1, PROMPT, HEAD_DIM),
    (1, ROWS, HEAD_DIM),
    (1, ROWS, HEAD_DIM),
    (1, 4, TREE, TREE),
)
TYPES = (jnp.bfloat16,) * 5 + (jnp.int32,)


def matmul_nt(a, b):
    return lax.dot_general(a, b, (((1,), (1,)), ((), ())), preferred_element_type=jnp.float32)


def attend_rows(first, rows, lag, held, o_ref, stacked, score, arrived):
    q_ref, k_ref, v_ref, tk_ref, tv_ref, mask_ref = held
    part_rows = TREE if rows % TREE == 0 else TREE // 2
    parts = rows // part_rows
    tiles = GROUP * rows // TILE
    per_part = tiles // parts
    blocks = PROMPT // KEY_BLOCK
    heads = TILE // part_rows
    copies = o_ref.shape[0]
    slots = lag + 1
    ones = jnp.ones((KEY_BLOCK, HEAD_DIM), jnp.bfloat16)
    arrived("queries")
    for p in range(parts):
        for g in range(GROUP):
            start = (p * GROUP + g) * part_rows
            row = first + p * part_rows
            stacked[start : start + part_rows, :] = q_ref[
                0, row : row + part_rows, g * HEAD_DIM : (g + 1) * HEAD_DIM
            ]

    ready = {}
    for t in range(tiles + lag):
        done = t - lag
        peak = None
        summed = None
        for b in range(blocks):
            keys = slice(b * KEY_BLOCK, (b + 1) * KEY_BLOCK)
            if t < tiles:
                if t == 0:
                    arrived("keys", b)
                s = matmul_nt(stacked[t * TILE : (t + 1) * TILE, :], k_ref[0, keys, :])
                score[t % slots, :, keys] = s
                for i in range(KEY_BLOCK // 128):
                    piece = s[:, i * 128 : (i + 1) * 128]
                    peak = piece if peak is None else jnp.maximum(peak, piece)
            if done >= 0:
                if done == 0 and b == 0:
                    arrived("values")
                weights = jnp.exp2(score[done % slots, :, keys] * EXP2_SCALE - ready[done][1]).astype(jnp.bfloat16)
                wide = jnp.concatenate([v_ref[0, keys, :], ones], axis=1)
                piece = jnp.dot(weights, wide, preferred_element_type=jnp.float32)
                summed = piece if summed is None else summed + piece
        if done >= 0:
            tree_scores, highest, batch = ready.pop(done)
            tree_exp = jnp.exp2(tree_scores * EXP2_SCALE - highest)
            totals = summed[:, HEAD_DIM:] + jnp.sum(tree_exp, axis=-1, keepdims=True)
            tree_values = tv_ref[0, batch * TREE : (batch + 1) * TREE, :]
            attended = summed[:, :HEAD_DIM] + jnp.dot(
                tree_exp.astype(jnp.bfloat16), tree_values, preferred_element_type=jnp.float32
            )
            attended = (attended / totals).astype(jnp.bfloat16)
            p, q = divmod(done, per_part)
            for i in range(heads):
                g = q * heads + i
                for c in range(copies):
                    o_ref[c, p * part_rows : (p + 1) * part_rows, g * HEAD_DIM : (g + 1) * HEAD_DIM] = attended[
                        i * part_rows : (i + 1) * part_rows
                    ]
        if t < tiles:
            if t == 0:
                arrived("tree")
            row = first + (t // per_part) * part_rows
            batch = row // TREE
            inside = row - batch * TREE
            seen = mask_ref[0, batch, inside : inside + part_rows, :]
            seen = jnp.concatenate([seen] * heads, axis=0) == 1
            tree_keys = tk_ref[0, batch * TREE : (batch + 1) * TREE, :]
            tree_scores = matmul_nt(stacked[t * TILE : (t + 1) * TILE, :], tree_keys)
            tree_scores = jnp.where(seen, tree_scores, -jnp.inf)
            highest = jnp.maximum(
                jnp.max(peak, axis=-1, keepdims=True), jnp.max(tree_scores, axis=-1, keepdims=True)
            )
            ready[t] = (tree_scores, highest * EXP2_SCALE, batch)


def attend_kernel(first, rows, lag, loaded, *refs):
    o_ref, stacked, score = refs[6:9]
    held = list(refs[:6])
    copies = {}
    if loaded:
        sem = refs[-1]
        for i, buffer in zip(loaded, refs[9:]):
            held[i] = buffer
        count = 0
        for i in (0, 1, 3, 5, 2, 4):
            if i not in loaded:
                continue
            pieces = [(refs[i], held[i])]
            if i == 0:
                pieces = [(refs[0].at[:, pl.ds(first, rows)], held[0].at[:, pl.ds(first, rows)])]
            if i == 1:
                blocks = [pl.ds(b * KEY_BLOCK, KEY_BLOCK) for b in range(PROMPT // KEY_BLOCK)]
                pieces = [(refs[1].at[:, keys], held[1].at[:, keys]) for keys in blocks]
            for b, (source, target) in enumerate(pieces):
                copies[i, b] = pltpu.make_async_copy(source, target, sem.at[count])
                copies[i, b].start()
                count += 1

    def arrived(what, b=0):
        for i in {"queries": (0,), "keys": (1,), "tree": (3, 5), "values": (2, 4)}[what]:
            if (i, b) in copies:
                copies[i, b].wait()

    attend_rows(first, rows, lag, held, o_ref, stacked, score, arrived)


def attend(arrays, first, rows, copies, loaded, limit):
    lag = 2 if 2 in loaded else 1
    vmem = pl.BlockSpec(memory_space=pltpu.VMEM)
    total_rows = GROUP * rows
    scratch = [
        pltpu.VMEM((total_rows, HEAD_DIM), jnp.bfloat16),
        pltpu.VMEM((lag + 1, TILE, PROMPT), jnp.float32),
    ]
    scratch += [pltpu.VMEM(SHAPES[i], TYPES[i]) for i in loaded]
    if loaded:
        scratch.append(pltpu.SemaphoreType.DMA((5 + PROMPT // KEY_BLOCK,)))
    return pl.pallas_call(
        functools.partial(attend_kernel, first, rows, lag, loaded),
        out_shape=jax.ShapeDtypeStruct((copies, rows, WIDTH), jnp.bfloat16),
        in_specs=[pl.BlockSpec(memory_space=pltpu.HBM) if i in loaded else vmem for i in range(6)],
        out_specs=vmem,
        scratch_shapes=scratch,
        compiler_params=pltpu.CompilerParams(vmem_limit_bytes=limit * 2**20),
        cost_estimate=pl.CostEstimate(
            flops=4 * total_rows * PROMPT * HEAD_DIM,
            bytes_accessed=3 * 2**20,
            transcendentals=total_rows * PROMPT,
        ),
        name=f"attend_{first}_{rows}",
    )(*arrays)


def place_kernel(first, rows, bounce, *refs):
    flip_ref, pieces_ref = refs[:2]
    out_ref, sem = (refs[-4], refs[-3]) if bounce else (refs[-2], refs[-1])
    if bounce:
        buffer, fetched = refs[-2:]
        fetches = [pltpu.make_async_copy(pieces_ref.at[j], buffer.at[j], fetched.at[j]) for j in range(8)]
        for fetch in fetches:
            fetch.start()
        pieces_ref = buffer
    copies = []
    for j in range(8):
        column = pl.multiple_of(lax.bitwise_xor(flip_ref[0], j) * WIDTH, WIDTH)
        copies.append(
            pltpu.make_async_copy(
                pieces_ref.at[j], out_ref.at[0, pl.ds(first, rows), pl.ds(column, WIDTH)], sem.at[j]
            )
        )
    for j, copy in enumerate(copies):
        if bounce:
            fetches[j].wait()
        copy.start()
    for copy in copies:
        copy.wait()


def place(pieces, flip, out, first, rows, bounce=False):
    operands = (flip, pieces) if out is None else (flip, pieces, out)
    return pl.pallas_call(
        functools.partial(place_kernel, first, rows, bounce),
        in_specs=[
            pl.BlockSpec(memory_space=pltpu.SMEM),
            pl.BlockSpec(memory_space=pl.ANY if bounce else pltpu.VMEM),
        ]
        + [pl.BlockSpec(memory_space=pl.ANY)] * (len(operands) - 2),
        out_specs=pl.BlockSpec(memory_space=pl.ANY),
        out_shape=jax.ShapeDtypeStruct((1, ROWS, 8 * WIDTH), jnp.bfloat16),
        scratch_shapes=[pltpu.SemaphoreType.DMA((8,))]
        + ([pltpu.VMEM(pieces.shape, pieces.dtype), pltpu.SemaphoreType.DMA((8,))] if bounce else []),
        input_output_aliases={} if out is None else {2: 0},
        compiler_params=pltpu.CompilerParams(vmem_limit_bytes=4 * 2**20),
        cost_estimate=pl.CostEstimate(flops=0, bytes_accessed=32 * rows * WIDTH, transcendentals=0),
        name=f"place_{first}",
    )(*operands)


def hand_on(block):
    route = []
    for s in range(64):
        for t in range(8):
            route.append((s * 8 + t, ((s + 1) % 64) * 8 + (t if s % 2 == 0 else t ^ 4)))
    return lax.ppermute(block, ("segment", "tensor"), route)


def fan_kernel(block_ref, out_ref, sem):
    copies = [pltpu.make_async_copy(block_ref.at[0], out_ref.at[j], sem.at[j]) for j in range(8)]
    for copy in copies:
        copy.start()
    for copy in copies:
        copy.wait()


def fan(block):
    return pl.pallas_call(
        fan_kernel,
        in_specs=[pl.BlockSpec(memory_space=pltpu.VMEM)],
        out_specs=pl.BlockSpec(memory_space=pl.ANY),
        out_shape=jax.ShapeDtypeStruct((8,) + block.shape[1:], block.dtype),
        scratch_shapes=[pltpu.SemaphoreType.DMA((8,))],
        compiler_params=pltpu.CompilerParams(vmem_limit_bytes=4 * 2**20),
        cost_estimate=pl.CostEstimate(flops=0, bytes_accessed=18 * block.size, transcendentals=0),
        name=f"fan_{block.shape[1]}",
    )(block)


CUT = 96


def spread(blocks):
    return lax.all_to_all(blocks, "tensor", 0, 0)


def body(*arrays):
    core = lax.bitwise_and(lax.axis_index("segment"), 1)
    flip = jnp.reshape((1 - core) * 4, (1,)).astype(jnp.int32)
    straight = jnp.zeros((1,), jnp.int32)
    barrier = lax.optimization_barrier
    a1 = attend(arrays, 0, CUT, 8, (0, 1, 2, 3, 4, 5), 60)
    g1 = spread(a1)
    a2 = attend(arrays, CUT, ROWS - CUT, 1, (3, 4, 5), 24)
    n2 = fan(hand_on(a2))
    n2, g1 = barrier((n2, g1))
    g2 = spread(n2)
    n1 = hand_on(g1)
    out = place(n1, straight, None, 0, CUT, bounce=True)
    return place(g2, flip, out, CUT, ROWS - CUT)


def solution(mesh):
    placed = (
        P("segment", None, "tensor"),
        P("segment", None, "tensor"),
        P("segment", None, "tensor"),
        P("segment", None, "tensor"),
        P("segment", None, "tensor"),
        P("segment", None, None, None),
    )
    return jax.shard_map(
        body, mesh=mesh, in_specs=placed, out_specs=P("segment", None, None), check_vma=False
    )
```

```python
import functools

import jax
import jax.numpy as jnp
from jax import lax
from jax.experimental import pallas as pl
from jax.experimental.pallas import tpu as pltpu
from jax.sharding import PartitionSpec as P

HEAD_DIM = 128
TREE = 64
PROMPT = 4096
GROUP = 8
ROWS = 256
WIDTH = GROUP * HEAD_DIM
EXP2_SCALE = 1.4426950408889634 * HEAD_DIM ** (-0.5)
TILE = 256
KEY_BLOCK = 1024
SHAPES = (
    (1, ROWS, WIDTH),
    (1, PROMPT, HEAD_DIM),
    (1, PROMPT, HEAD_DIM),
    (1, ROWS, HEAD_DIM),
    (1, ROWS, HEAD_DIM),
    (1, 4, TREE, TREE),
)
TYPES = (jnp.bfloat16,) * 5 + (jnp.int32,)


def matmul_nt(a, b):
    return lax.dot_general(a, b, (((1,), (1,)), ((), ())), preferred_element_type=jnp.float32)


def attend_rows(first, rows, lag, held, o_ref, stacked, score, arrived):
    q_ref, k_ref, v_ref, tk_ref, tv_ref, mask_ref = held
    part_rows = TREE if rows % TREE == 0 else TREE // 2
    parts = rows // part_rows
    tiles = GROUP * rows // TILE
    per_part = tiles // parts
    blocks = PROMPT // KEY_BLOCK
    heads = TILE // part_rows
    copies = o_ref.shape[0]
    slots = lag + 1
    arrived("queries")
    for p in range(parts):
        for g in range(GROUP):
            start = (p * GROUP + g) * part_rows
            row = first + p * part_rows
            stacked[start : start + part_rows, :] = q_ref[
                0, row : row + part_rows, g * HEAD_DIM : (g + 1) * HEAD_DIM
            ]

    ready = {}
    for t in range(tiles + lag):
        done = t - lag
        peak = None
        summed = None
        added = None
        for b in range(blocks):
            keys = slice(b * KEY_BLOCK, (b + 1) * KEY_BLOCK)
            if t < tiles:
                if t == 0:
                    arrived("keys", b)
                s = matmul_nt(stacked[t * TILE : (t + 1) * TILE, :], k_ref[0, keys, :])
                score[t % slots, :, keys] = s
                for i in range(KEY_BLOCK // 128):
                    piece = s[:, i * 128 : (i + 1) * 128]
                    peak = piece if peak is None else jnp.maximum(peak, piece)
            if done >= 0:
                if done == 0 and b == 0:
                    arrived("values")
                exps = jnp.exp2(score[done % slots, :, keys] * EXP2_SCALE - ready[done][1])
                for i in range(KEY_BLOCK // 128):
                    piece = exps[:, i * 128 : (i + 1) * 128]
                    added = piece if added is None else added + piece
                piece = jnp.dot(exps.astype(jnp.bfloat16), v_ref[0, keys, :], preferred_element_type=jnp.float32)
                summed = piece if summed is None else summed + piece
        if done >= 0:
            tree_scores, highest, batch = ready.pop(done)
            tree_exp = jnp.exp2(tree_scores * EXP2_SCALE - highest)
            totals = jnp.sum(added, axis=-1, keepdims=True) + jnp.sum(tree_exp, axis=-1, keepdims=True)
            tree_values = tv_ref[0, batch * TREE : (batch + 1) * TREE, :]
            attended = summed + jnp.dot(
                tree_exp.astype(jnp.bfloat16), tree_values, preferred_element_type=jnp.float32
            )
            attended = (attended / totals).astype(jnp.bfloat16)
            p, q = divmod(done, per_part)
            for i in range(heads):
                g = q * heads + i
                for c in range(copies):
                    o_ref[c, p * part_rows : (p + 1) * part_rows, g * HEAD_DIM : (g + 1) * HEAD_DIM] = attended[
                        i * part_rows : (i + 1) * part_rows
                    ]
        if t < tiles:
            if t == 0:
                arrived("tree")
            row = first + (t // per_part) * part_rows
            batch = row // TREE
            inside = row - batch * TREE
            seen = mask_ref[0, batch, inside : inside + part_rows, :]
            seen = jnp.concatenate([seen] * heads, axis=0) == 1
            tree_keys = tk_ref[0, batch * TREE : (batch + 1) * TREE, :]
            tree_scores = matmul_nt(stacked[t * TILE : (t + 1) * TILE, :], tree_keys)
            tree_scores = jnp.where(seen, tree_scores, -jnp.inf)
            highest = jnp.maximum(
                jnp.max(peak, axis=-1, keepdims=True), jnp.max(tree_scores, axis=-1, keepdims=True)
            )
            ready[t] = (tree_scores, highest * EXP2_SCALE, batch)


def attend_kernel(first, rows, lag, loaded, *refs):
    o_ref, stacked, score = refs[6:9]
    held = list(refs[:6])
    copies = {}
    if loaded:
        sem = refs[-1]
        for i, buffer in zip(loaded, refs[9:]):
            held[i] = buffer
        count = 0
        for i in (0, 1, 3, 5, 2, 4):
            if i not in loaded:
                continue
            pieces = [(refs[i], held[i])]
            if i == 0:
                pieces = [(refs[0].at[:, pl.ds(first, rows)], held[0].at[:, pl.ds(first, rows)])]
            if i == 1:
                blocks = [pl.ds(b * KEY_BLOCK, KEY_BLOCK) for b in range(PROMPT // KEY_BLOCK)]
                pieces = [(refs[1].at[:, keys], held[1].at[:, keys]) for keys in blocks]
            for b, (source, target) in enumerate(pieces):
                copies[i, b] = pltpu.make_async_copy(source, target, sem.at[count])
                copies[i, b].start()
                count += 1

    def arrived(what, b=0):
        for i in {"queries": (0,), "keys": (1,), "tree": (3, 5), "values": (2, 4)}[what]:
            if (i, b) in copies:
                copies[i, b].wait()

    attend_rows(first, rows, lag, held, o_ref, stacked, score, arrived)


def attend(arrays, first, rows, copies, loaded, limit):
    lag = 2 if 2 in loaded else 1
    vmem = pl.BlockSpec(memory_space=pltpu.VMEM)
    total_rows = GROUP * rows
    scratch = [
        pltpu.VMEM((total_rows, HEAD_DIM), jnp.bfloat16),
        pltpu.VMEM((lag + 1, TILE, PROMPT), jnp.float32),
    ]
    scratch += [pltpu.VMEM(SHAPES[i], TYPES[i]) for i in loaded]
    if loaded:
        scratch.append(pltpu.SemaphoreType.DMA((5 + PROMPT // KEY_BLOCK,)))
    return pl.pallas_call(
        functools.partial(attend_kernel, first, rows, lag, loaded),
        out_shape=jax.ShapeDtypeStruct((copies, rows, WIDTH), jnp.bfloat16),
        in_specs=[pl.BlockSpec(memory_space=pltpu.HBM) if i in loaded else vmem for i in range(6)],
        out_specs=vmem,
        scratch_shapes=scratch,
        compiler_params=pltpu.CompilerParams(vmem_limit_bytes=limit * 2**20),
        cost_estimate=pl.CostEstimate(
            flops=4 * total_rows * PROMPT * HEAD_DIM,
            bytes_accessed=3 * 2**20,
            transcendentals=total_rows * PROMPT,
        ),
        name=f"attend_{first}_{rows}",
    )(*arrays)


def place_kernel(first, rows, bounce, *refs):
    flip_ref, pieces_ref = refs[:2]
    out_ref, sem = (refs[-4], refs[-3]) if bounce else (refs[-2], refs[-1])
    if bounce:
        buffer, fetched = refs[-2:]
        fetches = [pltpu.make_async_copy(pieces_ref.at[j], buffer.at[j], fetched.at[j]) for j in range(8)]
        for fetch in fetches:
            fetch.start()
        pieces_ref = buffer
    copies = []
    for j in range(8):
        column = pl.multiple_of(lax.bitwise_xor(flip_ref[0], j) * WIDTH, WIDTH)
        copies.append(
            pltpu.make_async_copy(
                pieces_ref.at[j], out_ref.at[0, pl.ds(first, rows), pl.ds(column, WIDTH)], sem.at[j]
            )
        )
    for j, copy in enumerate(copies):
        if bounce:
            fetches[j].wait()
        copy.start()
    for copy in copies:
        copy.wait()


def place(pieces, flip, out, first, rows, bounce=False):
    operands = (flip, pieces) if out is None else (flip, pieces, out)
    return pl.pallas_call(
        functools.partial(place_kernel, first, rows, bounce),
        in_specs=[
            pl.BlockSpec(memory_space=pltpu.SMEM),
            pl.BlockSpec(memory_space=pl.ANY if bounce else pltpu.VMEM),
        ]
        + [pl.BlockSpec(memory_space=pl.ANY)] * (len(operands) - 2),
        out_specs=pl.BlockSpec(memory_space=pl.ANY),
        out_shape=jax.ShapeDtypeStruct((1, ROWS, 8 * WIDTH), jnp.bfloat16),
        scratch_shapes=[pltpu.SemaphoreType.DMA((8,))]
        + ([pltpu.VMEM(pieces.shape, pieces.dtype), pltpu.SemaphoreType.DMA((8,))] if bounce else []),
        input_output_aliases={} if out is None else {2: 0},
        compiler_params=pltpu.CompilerParams(vmem_limit_bytes=4 * 2**20),
        cost_estimate=pl.CostEstimate(flops=0, bytes_accessed=32 * rows * WIDTH, transcendentals=0),
        name=f"place_{first}",
    )(*operands)


def hand_on(block):
    route = []
    for s in range(64):
        for t in range(8):
            route.append((s * 8 + t, ((s + 1) % 64) * 8 + (t if s % 2 == 0 else t ^ 4)))
    return lax.ppermute(block, ("segment", "tensor"), route)


def fan_kernel(block_ref, out_ref, sem):
    copies = [pltpu.make_async_copy(block_ref.at[0], out_ref.at[j], sem.at[j]) for j in range(8)]
    for copy in copies:
        copy.start()
    for copy in copies:
        copy.wait()


def fan(block):
    return pl.pallas_call(
        fan_kernel,
        in_specs=[pl.BlockSpec(memory_space=pltpu.VMEM)],
        out_specs=pl.BlockSpec(memory_space=pl.ANY),
        out_shape=jax.ShapeDtypeStruct((8,) + block.shape[1:], block.dtype),
        scratch_shapes=[pltpu.SemaphoreType.DMA((8,))],
        compiler_params=pltpu.CompilerParams(vmem_limit_bytes=4 * 2**20),
        cost_estimate=pl.CostEstimate(flops=0, bytes_accessed=18 * block.size, transcendentals=0),
        name=f"fan_{block.shape[1]}",
    )(block)


CUT = 96


def spread(blocks):
    return lax.all_to_all(blocks, "tensor", 0, 0)


def body(*arrays):
    core = lax.bitwise_and(lax.axis_index("segment"), 1)
    flip = jnp.reshape((1 - core) * 4, (1,)).astype(jnp.int32)
    straight = jnp.zeros((1,), jnp.int32)
    barrier = lax.optimization_barrier
    a1 = attend(arrays, 0, CUT, 8, (0, 1, 2, 3, 4, 5), 60)
    g1 = spread(a1)
    a2 = attend(arrays, CUT, ROWS - CUT, 1, (3, 4, 5), 24)
    n2 = fan(hand_on(a2))
    n2, g1 = barrier((n2, g1))
    g2 = spread(n2)
    n1 = hand_on(g1)
    out = place(n1, straight, None, 0, CUT, bounce=True)
    return place(g2, flip, out, CUT, ROWS - CUT)


def solution(mesh):
    placed = (
        P("segment", None, "tensor"),
        P("segment", None, "tensor"),
        P("segment", None, "tensor"),
        P("segment", None, "tensor"),
        P("segment", None, "tensor"),
        P("segment", None, None, None),
    )
    return jax.shard_map(
        body, mesh=mesh, in_specs=placed, out_specs=P("segment", None, None), check_vma=False
    )
```

```python
import functools

import jax
import jax.numpy as jnp
from jax import lax
from jax.experimental import pallas as pl
from jax.experimental.pallas import tpu as pltpu
from jax.sharding import PartitionSpec as P

HEAD_DIM = 128
TREE = 64
PROMPT = 4096
GROUP = 8
ROWS = 256
WIDTH = GROUP * HEAD_DIM
EXP2_SCALE = 1.4426950408889634 * HEAD_DIM ** (-0.5)
TILE = 256
KEY_BLOCK = 1024
SHAPES = (
    (1, ROWS, WIDTH),
    (1, PROMPT, HEAD_DIM),
    (1, PROMPT, HEAD_DIM),
    (1, ROWS, HEAD_DIM),
    (1, ROWS, HEAD_DIM),
    (1, 4, TREE, TREE),
)
TYPES = (jnp.bfloat16,) * 5 + (jnp.int32,)


def matmul_nt(a, b):
    return lax.dot_general(a, b, (((1,), (1,)), ((), ())), preferred_element_type=jnp.float32)


def attend_rows(first, rows, lag, held, o_ref, stacked, score, arrived):
    q_ref, k_ref, v_ref, tk_ref, tv_ref, mask_ref = held
    part_rows = TREE if rows % TREE == 0 else TREE // 2
    parts = rows // part_rows
    tiles = GROUP * rows // TILE
    per_part = tiles // parts
    blocks = PROMPT // KEY_BLOCK
    heads = TILE // part_rows
    copies = o_ref.shape[0]
    slots = lag + 1
    arrived("queries")
    for p in range(parts):
        for g in range(GROUP):
            start = (p * GROUP + g) * part_rows
            row = first + p * part_rows
            stacked[start : start + part_rows, :] = q_ref[
                0, row : row + part_rows, g * HEAD_DIM : (g + 1) * HEAD_DIM
            ]

    ready = {}
    for t in range(tiles + lag):
        done = t - lag
        peak = None
        summed = None
        added = None
        for b in range(blocks):
            keys = slice(b * KEY_BLOCK, (b + 1) * KEY_BLOCK)
            if t < tiles:
                if t == 0:
                    arrived("keys", b)
                s = matmul_nt(stacked[t * TILE : (t + 1) * TILE, :], k_ref[0, keys, :])
                score[t % slots, :, keys] = s
                for i in range(KEY_BLOCK // 128):
                    piece = s[:, i * 128 : (i + 1) * 128]
                    peak = piece if peak is None else jnp.maximum(peak, piece)
            if done >= 0:
                if done == 0 and b == 0:
                    arrived("values")
                exps = jnp.exp2(score[done % slots, :, keys] * EXP2_SCALE - ready[done][1])
                for i in range(KEY_BLOCK // 128):
                    piece = exps[:, i * 128 : (i + 1) * 128]
                    added = piece if added is None else added + piece
                piece = jnp.dot(exps.astype(jnp.bfloat16), v_ref[0, keys, :], preferred_element_type=jnp.float32)
                summed = piece if summed is None else summed + piece
        if done >= 0:
            tree_scores, highest, batch = ready.pop(done)
            tree_exp = jnp.exp2(tree_scores * EXP2_SCALE - highest)
            totals = jnp.sum(added, axis=-1, keepdims=True) + jnp.sum(tree_exp, axis=-1, keepdims=True)
            tree_values = tv_ref[0, batch * TREE : (batch + 1) * TREE, :]
            attended = summed + jnp.dot(
                tree_exp.astype(jnp.bfloat16), tree_values, preferred_element_type=jnp.float32
            )
            attended = (attended / totals).astype(jnp.bfloat16)
            p, q = divmod(done, per_part)
            for i in range(heads):
                g = q * heads + i
                for c in range(copies):
                    o_ref[c, p * part_rows : (p + 1) * part_rows, g * HEAD_DIM : (g + 1) * HEAD_DIM] = attended[
                        i * part_rows : (i + 1) * part_rows
                    ]
        if t < tiles:
            if t == 0:
                arrived("tree")
            row = first + (t // per_part) * part_rows
            batch = row // TREE
            inside = row - batch * TREE
            seen = mask_ref[0, batch, inside : inside + part_rows, :]
            seen = jnp.concatenate([seen] * heads, axis=0) == 1
            tree_keys = tk_ref[0, batch * TREE : (batch + 1) * TREE, :]
            tree_scores = matmul_nt(stacked[t * TILE : (t + 1) * TILE, :], tree_keys)
            tree_scores = jnp.where(seen, tree_scores, -jnp.inf)
            highest = jnp.maximum(
                jnp.max(peak, axis=-1, keepdims=True), jnp.max(tree_scores, axis=-1, keepdims=True)
            )
            ready[t] = (tree_scores, highest * EXP2_SCALE, batch)


def attend_kernel(first, rows, lag, loaded, *refs):
    o_ref, stacked, score = refs[6:9]
    held = list(refs[:6])
    copies = {}
    if loaded:
        sem = refs[-1]
        for i, buffer in zip(loaded, refs[9:]):
            held[i] = buffer
        count = 0
        for i in (0, 1, 3, 5, 2, 4):
            if i not in loaded:
                continue
            pieces = [(refs[i], held[i])]
            if i == 0:
                pieces = [(refs[0].at[:, pl.ds(first, rows)], held[0].at[:, pl.ds(first, rows)])]
            if i == 1:
                blocks = [pl.ds(b * KEY_BLOCK, KEY_BLOCK) for b in range(PROMPT // KEY_BLOCK)]
                pieces = [(refs[1].at[:, keys], held[1].at[:, keys]) for keys in blocks]
            for b, (source, target) in enumerate(pieces):
                copies[i, b] = pltpu.make_async_copy(source, target, sem.at[count])
                copies[i, b].start()
                count += 1

    def arrived(what, b=0):
        for i in {"queries": (0,), "keys": (1,), "tree": (3, 5), "values": (2, 4)}[what]:
            if (i, b) in copies:
                copies[i, b].wait()

    attend_rows(first, rows, lag, held, o_ref, stacked, score, arrived)


def attend(arrays, first, rows, copies, loaded, limit):
    lag = 2 if 2 in loaded else 1
    vmem = pl.BlockSpec(memory_space=pltpu.VMEM)
    total_rows = GROUP * rows
    scratch = [
        pltpu.VMEM((total_rows, HEAD_DIM), jnp.bfloat16),
        pltpu.VMEM((lag + 1, TILE, PROMPT), jnp.float32),
    ]
    scratch += [pltpu.VMEM(SHAPES[i], TYPES[i]) for i in loaded]
    if loaded:
        scratch.append(pltpu.SemaphoreType.DMA((5 + PROMPT // KEY_BLOCK,)))
    return pl.pallas_call(
        functools.partial(attend_kernel, first, rows, lag, loaded),
        out_shape=jax.ShapeDtypeStruct((copies, rows, WIDTH), jnp.bfloat16),
        in_specs=[pl.BlockSpec(memory_space=pltpu.HBM) if i in loaded else vmem for i in range(6)],
        out_specs=vmem,
        scratch_shapes=scratch,
        compiler_params=pltpu.CompilerParams(vmem_limit_bytes=limit * 2**20),
        cost_estimate=pl.CostEstimate(
            flops=4 * total_rows * PROMPT * HEAD_DIM,
            bytes_accessed=3 * 2**20,
            transcendentals=total_rows * PROMPT,
        ),
        name=f"attend_{first}_{rows}",
    )(*arrays)


def place_kernel(first, rows, bounce, *refs):
    flip_ref, pieces_ref = refs[:2]
    out_ref, sem = (refs[-4], refs[-3]) if bounce else (refs[-2], refs[-1])
    half = rows // 2
    parts = [(j, h) for j in range(8) for h in range(2)]
    fetches = []
    if bounce:
        buffer, fetched = refs[-2:]
        for j, h in parts:
            piece = (j, pl.ds(h * half, half))
            fetches.append(pltpu.make_async_copy(pieces_ref.at[piece], buffer.at[piece], fetched.at[2 * j + h]))
        for fetch in fetches:
            fetch.start()
        pieces_ref = buffer
    copies = []
    for j, h in parts:
        column = pl.multiple_of(lax.bitwise_xor(flip_ref[0], j) * WIDTH, WIDTH)
        copies.append(
            pltpu.make_async_copy(
                pieces_ref.at[j, pl.ds(h * half, half)],
                out_ref.at[0, pl.ds(first + h * half, half), pl.ds(column, WIDTH)],
                sem.at[2 * j + h],
            )
        )
    for i, copy in enumerate(copies):
        if bounce:
            fetches[i].wait()
        copy.start()
    for copy in copies:
        copy.wait()


def place(pieces, flip, out, first, rows, bounce=False):
    operands = (flip, pieces) if out is None else (flip, pieces, out)
    return pl.pallas_call(
        functools.partial(place_kernel, first, rows, bounce),
        in_specs=[
            pl.BlockSpec(memory_space=pltpu.SMEM),
            pl.BlockSpec(memory_space=pl.ANY if bounce else pltpu.VMEM),
        ]
        + [pl.BlockSpec(memory_space=pl.ANY)] * (len(operands) - 2),
        out_specs=pl.BlockSpec(memory_space=pl.ANY),
        out_shape=jax.ShapeDtypeStruct((1, ROWS, 8 * WIDTH), jnp.bfloat16),
        scratch_shapes=[pltpu.SemaphoreType.DMA((16,))]
        + ([pltpu.VMEM(pieces.shape, pieces.dtype), pltpu.SemaphoreType.DMA((16,))] if bounce else []),
        input_output_aliases={} if out is None else {2: 0},
        compiler_params=pltpu.CompilerParams(vmem_limit_bytes=4 * 2**20),
        cost_estimate=pl.CostEstimate(flops=0, bytes_accessed=32 * rows * WIDTH, transcendentals=0),
        name=f"place_{first}",
    )(*operands)


def hand_on(block):
    route = []
    for s in range(64):
        for t in range(8):
            route.append((s * 8 + t, ((s + 1) % 64) * 8 + (t if s % 2 == 0 else t ^ 4)))
    return lax.ppermute(block, ("segment", "tensor"), route)


def fan_kernel(block_ref, out_ref, sem):
    copies = [pltpu.make_async_copy(block_ref.at[0], out_ref.at[j], sem.at[j]) for j in range(8)]
    for copy in copies:
        copy.start()
    for copy in copies:
        copy.wait()


def fan(block):
    return pl.pallas_call(
        fan_kernel,
        in_specs=[pl.BlockSpec(memory_space=pltpu.VMEM)],
        out_specs=pl.BlockSpec(memory_space=pl.ANY),
        out_shape=jax.ShapeDtypeStruct((8,) + block.shape[1:], block.dtype),
        scratch_shapes=[pltpu.SemaphoreType.DMA((8,))],
        compiler_params=pltpu.CompilerParams(vmem_limit_bytes=4 * 2**20),
        cost_estimate=pl.CostEstimate(flops=0, bytes_accessed=18 * block.size, transcendentals=0),
        name=f"fan_{block.shape[1]}",
    )(block)


CUT = 96


def spread(blocks):
    return lax.all_to_all(blocks, "tensor", 0, 0)


def body(*arrays):
    core = lax.bitwise_and(lax.axis_index("segment"), 1)
    flip = jnp.reshape((1 - core) * 4, (1,)).astype(jnp.int32)
    straight = jnp.zeros((1,), jnp.int32)
    barrier = lax.optimization_barrier
    a1 = attend(arrays, 0, CUT, 8, (0, 1, 2, 3, 4, 5), 60)
    g1 = spread(a1)
    a2 = attend(arrays, CUT, ROWS - CUT, 1, (3, 4, 5), 24)
    n2 = fan(hand_on(a2))
    n2, g1 = barrier((n2, g1))
    g2 = spread(n2)
    n1 = hand_on(g1)
    out = place(n1, straight, None, 0, CUT, bounce=True)
    return place(g2, flip, out, CUT, ROWS - CUT)


def solution(mesh):
    placed = (
        P("segment", None, "tensor"),
        P("segment", None, "tensor"),
        P("segment", None, "tensor"),
        P("segment", None, "tensor"),
        P("segment", None, "tensor"),
        P("segment", None, None, None),
    )
    return jax.shard_map(
        body, mesh=mesh, in_specs=placed, out_specs=P("segment", None, None), check_vma=False
    )
```
